32 devices in a mesh: row: 4 (over z), col: 4 (over x, core), grp: 2 (over y).
Axes of the slice: x: 2, y: 2, z: 4, core: 2. Of those that a mesh axis runs over, the one named last changes fastest.
Arguments:
- matrix: float32 [16384, 16384], P('row', ('col', 'grp')), may hold values from -8 to 8, as said below
- basis_rows: float32 [4096, 16384], P(('col', 'grp'), 'row'), may hold values from -6 to 6
- reflectors: float32 [16384, 512], P('row'), may hold values from -0.125 to 0.125
- tfactor: float32 [512, 512], replicated, may hold values from -0.25 to 2, as said below
Outputs:
- new_matrix: float32 [16384, 16384], P('row', ('col', 'grp'))
- new_basis: float32 [4096, 16384], P(('col', 'grp'), 'row')
The draws below stay inside these ranges and needn't reach their ends.
Inputs may be any that keep to these rules, and one draw needn't show every extreme that they name: The matrix A that it represents is symmetric. `tfactor`: upper triangular: zero below the diagonal, diagonal between 1 and 2.
All inputs are finite; a program needn't handle non-finite values.
Results may differ from the reference program's by a relative error of at most 0.000073.
Values sent between devices are 32-bit elements; how exact they have to be, the bound alone decides.
A program may use at most 192 MiB of HBM per device.

```python
import jax
import jax.numpy as jnp
from jax import lax

M = 16384
NB = 512
ROWBLK = 4096
COLBLK = 2048
SLICE = 512
QROWS = 4096


def draw_matrix(key, part):
    first_key = jax.random.fold_in(key, 11)
    normal = jax.random.normal(first_key, (M, M), jnp.float32)
    symmetric = (normal + normal.T) * 0.70710678
    symmetric = jnp.clip(symmetric, -8.0, 8.0)
    nrow = M // ROWBLK
    ncol = M // COLBLK
    return symmetric.reshape(M, nrow, ncol, SLICE).transpose(0, 2, 1, 3).reshape(M, M)


def draw_tfactor(key, part):
    first_key = jax.random.fold_in(key, 21)
    second_key = jax.random.fold_in(key, 22)
    above = jnp.clip(jax.random.normal(first_key, (NB, NB), jnp.float32) * NB ** (-0.5), -0.25, 0.25)
    diag = jax.random.uniform(second_key, (NB,), jnp.float32, 1.0, 2.0)
    return jnp.triu(above, 1) + jnp.diag(diag)


def shard_levels(own_key, extent, shards, least, top_value):
    level, own = 1.0, jax.random.fold_in(own_key, 6)
    for dim, shards_of in shards:
        heights = jnp.exp(jax.random.uniform(jax.random.fold_in(own, dim), (shards_of,), jnp.float32, least / len(shards), top_value / len(shards)))
        level = level * jnp.repeat(heights, extent[dim] // shards_of).reshape([-1 if axis == dim else 1 for axis in range(len(extent))])
    return level


def gaussian(own_key, dims, deviation, most, pieces=(), held_as=jnp.bfloat16):
    loudness = shard_levels(own_key, dims, pieces, -0.22, 0.18) if pieces else 1.0
    array = jax.random.normal(own_key, dims, jnp.float32) * deviation * loudness
    return jnp.minimum(jnp.maximum(array, -most), most).astype(held_as)


def setup_inputs(seed: int = 0) -> dict:
    splits = jax.random.split(jax.random.key(seed), 5)
    return {
        "matrix": draw_matrix(jax.random.fold_in(splits[4], 71), 0),
        "basis_rows": gaussian(splits[1], (QROWS, M), 1.0, 6.0, ((0, 8), (1, 4)), jnp.float32),
        "reflectors": gaussian(splits[2], (M, NB), (4 * NB) ** -0.5, 0.125, ((0, 4),), jnp.float32),
        "tfactor": draw_tfactor(jax.random.fold_in(splits[4], 71), 0),
    }


def to_global(stored):
    nrow = M // ROWBLK
    ncol = M // COLBLK
    return stored.reshape(M, ncol, nrow, SLICE).transpose(0, 2, 1, 3).reshape(M, M)


def to_stored(full):
    nrow = M // ROWBLK
    ncol = M // COLBLK
    return full.reshape(M, nrow, ncol, SLICE).transpose(0, 2, 1, 3).reshape(M, M)


def reference(matrix, basis_rows, reflectors, tfactor):
    highest = lax.Precision.HIGHEST
    full = to_global(matrix)
    applied = jnp.dot(full, reflectors, precision=highest, preferred_element_type=jnp.float32)
    wide = jnp.dot(applied, tfactor, precision=highest, preferred_element_type=jnp.float32)
    cross = jnp.dot(reflectors.T, wide, precision=highest, preferred_element_type=jnp.float32)
    inner = jnp.dot(tfactor.T, cross, precision=highest, preferred_element_type=jnp.float32)
    zeta = wide - 0.5 * jnp.dot(reflectors, inner, precision=highest, preferred_element_type=jnp.float32)
    updated = full - jnp.dot(reflectors, zeta.T, precision=highest, preferred_element_type=jnp.float32)
    updated = updated - jnp.dot(zeta, reflectors.T, precision=highest, preferred_element_type=jnp.float32)
    q_proj = jnp.dot(basis_rows, reflectors, precision=highest, preferred_element_type=jnp.float32)
    q_fact = jnp.dot(q_proj, tfactor, precision=highest, preferred_element_type=jnp.float32)
    new_basis = basis_rows - jnp.dot(q_fact, reflectors.T, precision=highest, preferred_element_type=jnp.float32)
    return to_stored(updated), new_basis
```

```python
import jax
import jax.numpy as jnp
from jax import lax
from jax.experimental import pallas as pl
from jax.experimental.pallas import tpu as pltpu
from jax.sharding import PartitionSpec as P


def halves(x):
    high = x.astype(jnp.bfloat16)
    return high, (x - high.astype(jnp.float32)).astype(jnp.bfloat16)


def apply_kernel(index_ref, a_ref, v_ref, *rest):
    out_ref = rest[-1]
    a_high, a_low = halves(a_ref[...])
    v_high, v_low = halves(v_ref[...])
    product = jnp.dot(
        jnp.concatenate([a_high, a_low, a_high], axis=1),
        jnp.concatenate([v_high, v_high, v_low], axis=0),
        preferred_element_type=jnp.float32,
    )
    out_ref[...] = product if len(rest) == 1 else rest[0][...] + product


def apply_chunk(matrix, chunk, total, index):
    rows, (depth, wide) = matrix.shape[0], chunk.shape
    tile = min(512, rows)
    specs = [
        pl.BlockSpec((tile, depth), lambda i, c: (i, c[0])),
        pl.BlockSpec((depth, wide), lambda i, c: (0, 0)),
    ]
    args = [matrix, chunk]
    if total is not None:
        specs.append(pl.BlockSpec((tile, wide), lambda i, c: (i, 0)))
        args.append(total)
    return pl.pallas_call(
        apply_kernel,
        out_shape=jax.ShapeDtypeStruct((rows, wide), jnp.float32),
        grid_spec=pltpu.PrefetchScalarGridSpec(
            num_scalar_prefetch=1,
            grid=(rows // tile,),
            in_specs=specs,
            out_specs=pl.BlockSpec((tile, wide), lambda i, c: (i, 0)),
        ),
        cost_estimate=pl.CostEstimate(
            flops=6 * rows * depth * wide,
            bytes_accessed=4 * rows * (depth + 2 * wide),
            transcendentals=0,
        ),
        name="apply_chunk",
    )(index, *args)


def update_kernel(order_ref, a_ref, near_ref, far_ref, vr_ref, vc_ref, zc_ref, *rest):
    out_ref, right = rest[-2:]

    @pl.when(pl.program_id(0) == 0)
    def _():
        v_high, v_low = halves(vc_ref[...])
        z_high, z_low = halves(zc_ref[...])
        right[...] = jnp.concatenate([v_high, v_high, v_low, z_high, z_high, z_low], axis=1)

    first = pl.program_id(0) < pl.num_programs(0) // 2
    w_high, w_low = halves(jnp.where(first, near_ref[...], far_ref[...]))
    v_high, v_low = halves(vr_ref[...])
    left = jnp.concatenate([w_high, w_low, w_high, v_high, v_low, v_high], axis=1)
    out_ref[...] = a_ref[...] - lax.dot_general(
        left, right[...], (((1,), (1,)), ((), ())), preferred_element_type=jnp.float32
    )


def update_chunk(matrix, w_near, w_far, v_row, v_chunk, z_chunk, order, out):
    rows, (depth, wide) = matrix.shape[0], v_chunk.shape
    steps = order.shape[0] - 1
    tile, half = rows // steps, steps // 2
    specs = [
        pl.BlockSpec((tile, depth), lambda i, c: (c[i + 1], c[0])),
        pl.BlockSpec((tile, wide), lambda i, c: (jnp.minimum(i, half - 1), 0)),
        pl.BlockSpec((tile, wide), lambda i, c: (jnp.maximum(i - half, 0), 0)),
        pl.BlockSpec((tile, wide), lambda i, c: (c[i + 1], 0)),
        pl.BlockSpec((depth, wide), lambda i, c: (0, 0)),
        pl.BlockSpec((depth, wide), lambda i, c: (0, 0)),
    ]
    args = [matrix, w_near, w_far, v_row, v_chunk, z_chunk]
    alias = {}
    if out is not None:
        specs.append(pl.BlockSpec(memory_space=pl.ANY))
        args.append(out)
        alias = {7: 0}
    return pl.pallas_call(
        update_kernel,
        out_shape=jax.ShapeDtypeStruct(matrix.shape, jnp.float32),
        grid_spec=pltpu.PrefetchScalarGridSpec(
            num_scalar_prefetch=1,
            grid=(steps,),
            in_specs=specs,
            out_specs=pl.BlockSpec((tile, depth), lambda i, c: (c[i + 1], c[0])),
            scratch_shapes=[pltpu.VMEM((depth, 6 * wide), jnp.bfloat16)],
        ),
        input_output_aliases=alias,
        cost_estimate=pl.CostEstimate(
            flops=12 * rows * depth * wide,
            bytes_accessed=8 * rows * (depth + wide),
            transcendentals=0,
        ),
        name="update_chunk",
    )(order, *args)


def dot(a, b):
    return jnp.dot(a, b, precision=lax.Precision.HIGH, preferred_element_type=jnp.float32)


def swap(x, axis, bit):
    count = lax.axis_size(axis)
    return lax.ppermute(x, axis, [(i, i ^ bit) for i in range(count)])


def pick(x, index, axis):
    return lax.dynamic_index_in_dim(x, index, axis, keepdims=False)


def scatter_sum(total):
    if lax.axis_size("col") != 4 or lax.axis_size("grp") != 2:
        return lax.psum_scatter(total, ("col", "grp"), scatter_dimension=0, tiled=True)
    col, y = lax.axis_index("col"), lax.axis_index("grp")
    x, core = col // 2, col % 2
    depth, wide = total.shape[0] // 8, total.shape[1]
    total = total.reshape(2, 2, 2, depth, wide)
    mine = pick(total, core, 1) + swap(pick(total, 1 - core, 1), "col", 1)
    near, far = mine[:, :, : depth // 2], mine[:, :, depth // 2 :]
    near_in = swap(pick(near, 1 - x, 0), "col", 2)
    far_in = swap(pick(far, 1 - y, 1), "grp", 1)
    near = pick(near, x, 0) + near_in
    far = pick(far, y, 1) + far_in
    near_in = swap(pick(near, 1 - y, 0), "grp", 1)
    far_in = swap(pick(far, 1 - x, 0), "col", 2)
    return jnp.concatenate([pick(near, y, 0) + near_in, pick(far, x, 0) + far_in], axis=0)


def gather_rows(own):
    if lax.axis_size("col") != 4 or lax.axis_size("grp") != 2:
        whole = lax.all_gather(own, ("col", "grp"), axis=0, tiled=True)
        half = whole.shape[0] // 2
        tiles = jnp.arange(whole.shape[0] // own.shape[0])
        return whole[:half], whole[half:], tiles
    depth, _ = own.shape
    near, far = own[None, : depth // 2], own[None, depth // 2 :]
    near = jnp.concatenate([near, swap(near, "grp", 1)])
    far = jnp.concatenate([far, swap(far, "col", 2)])
    near_in, far_in = swap(near, "col", 2), swap(far, "grp", 1)
    near = jnp.concatenate([near, near_in])
    tiles = []
    for tile in range(4):
        source, place = (far, far_in)[tile % 2], tile // 2
        tiles += [near[tile], source[place]]
    mine = jnp.concatenate(tiles, axis=0)
    col, y = lax.axis_index("col"), lax.axis_index("grp")
    bits = jnp.arange(8)
    cols = col ^ (2 * (bits // 2 % 2) + bits // 4)
    rest = swap(mine, "col", 1)
    return mine, rest, cols * 2 + (y ^ (bits % 2))


def step(matrix, basis_rows, reflectors, tfactor):
    plane = ("col", "grp")
    member, groups = lax.axis_index(plane), lax.axis_size(plane)
    row, count = lax.axis_index("row"), lax.axis_size("row")
    ring = [(i, (i + 1) % count) for i in range(count)]
    slice_rows = reflectors.shape[0] // groups
    own_v = lax.dynamic_slice_in_dim(reflectors, member * slice_rows, slice_rows, 0)

    v_chunks, owners = [own_v], []
    for step in range(count):
        owners.append(((row - step + count) % count).astype(jnp.int32).reshape(1))
        if step + 1 < count:
            v_chunks.append(lax.ppermute(v_chunks[-1], "row", ring))
    total = apply_chunk(matrix, own_v, None, owners[0])
    total, q_proj = lax.optimization_barrier((total, dot(basis_rows, reflectors)))
    q_proj = lax.psum(q_proj, "row")
    for chunk, owner in zip(v_chunks[1:], owners[1:]):
        total = apply_chunk(matrix, chunk, total, owner)

    cross, total = lax.optimization_barrier((dot(reflectors.T, total), total))
    cross = lax.psum_scatter(cross, plane, scatter_dimension=0, tiled=True)
    applied = scatter_sum(total)
    w_slice = dot(applied, tfactor)
    cross, w_slice = lax.optimization_barrier((cross, w_slice))
    cross = lax.all_gather(lax.psum(cross, "row"), plane, axis=0, tiled=True)
    w_chunks = [w_slice]
    for _ in range(count - 1):
        w_chunks.append(lax.ppermute(w_chunks[-1], "row", ring))
    w_near, w_far, tiles = gather_rows(w_slice)
    inner = dot(tfactor.T, dot(cross, tfactor))

    out = None
    for v_chunk, w_chunk, owner in zip(v_chunks, w_chunks, owners):
        if out is not None:
            out, w_chunk = lax.optimization_barrier((out, w_chunk))
        z_chunk = w_chunk - dot(v_chunk, inner.T)
        order = jnp.concatenate([owner, tiles.astype(jnp.int32)])
        out = update_chunk(matrix, w_near, w_far, reflectors, v_chunk, z_chunk, order, out)

    new_basis = basis_rows - dot(dot(q_proj, tfactor), reflectors.T)
    return (out, new_basis)


def solution(mesh):
    placed = (P("row", ("col", "grp")), P(("col", "grp"), "row"), P("row", None), P())
    return jax.shard_map(
        step,
        mesh=mesh,
        in_specs=placed,
        out_specs=(P("row", ("col", "grp")), P(("col", "grp"), "row")),
        check_vma=False,
    )
```
